32 devices in a mesh: px: 8 (over z, y), py: 4 (over x, core).
Axes of the slice: x: 2, y: 2, z: 4, core: 2. Of those that a mesh axis runs over, the one named last changes fastest.
Arguments:
- history: bfloat16 [8, 4, 3, 128, 384], P('px', 'py'), may hold values from -6 to 6
- incident: float32 [8, 4, 4, 128, 384], P('px', 'py'), may hold values from -6 to 6
- blocks: bfloat16 [8, 4, 32, 128, 128], P('px', 'py'), may hold values from -0.09375 to 0.09375
- self_inverse: float32 [8, 4, 128, 128], P('px', 'py'), as said below
- neighbour: int32 [8, 4, 32], P('px', 'py'), may hold values from 0 to 8
- delay: int32 [8, 4, 32], P('px', 'py'), may hold values from 1 to 3
Outputs:
- currents: bfloat16 [8, 4, 4, 128, 384], P('px', 'py')
The draws below stay inside these ranges and needn't reach their ends.
Inputs may be any that keep to these rules, and one draw needn't show every extreme that they name: neighbour n names the source tile at row offset n // 3 - 1 and column offset n % 3 - 1. `self_inverse`: each matrix has a positive diagonal.
All inputs are finite; a program needn't handle non-finite values.
Results may differ from the reference program's by a relative error of at most 0.004.
Values may be sent and summed in bfloat16 or wider, within the bound.
A program may use at most 64 MiB of HBM per device.

```python
import jax
import jax.numpy as jnp
from jax import lax

B = 128
P_SIZE = 384
NBLK = 32
DMAX = 3
STEPS = 4
NTX = 8
NTY = 4


def draw_self_inverse(key, part):
    first, second = jax.random.split(jax.random.fold_in(key, 17))
    shape = (NTX, NTY, B, B)
    diag = jax.random.uniform(first, (NTX, NTY, B), jnp.float32, 0.6, 1.4)
    off = jax.random.normal(second, shape, jnp.float32) * (0.5 / B ** 0.5)
    eye = jnp.eye(B, dtype=jnp.float32)
    return off * (1.0 - eye) + diag[..., None] * eye


def plant(array, stream_key, least, high):
    longest = array.shape.index(max(array.shape))
    spots = []
    for shift in (0, 1):
        where = [jax.random.randint(jax.random.fold_in(stream_key, axis), (), 0, length) for axis, length in enumerate(array.shape)]
        where[longest] = (where[longest] + shift) % array.shape[longest]
        spots.append(tuple(where))
    return array.at[spots[0]].set(least).at[spots[1]].set(high)


def level_of(key, dims, cuts, least, largest):
    def one(position, parts):
        heights = jax.random.uniform(jax.random.fold_in(jax.random.fold_in(key, 6), position), (parts,), jnp.float32, least / len(cuts), largest / len(cuts))
        return jnp.repeat(jnp.exp(heights), dims[position] // parts).reshape((-1,) + (1,) * (len(dims) - position - 1))

    level = one(*cuts[0])
    for cut in cuts[1:]:
        level = level * one(*cut)
    return level


def gaussian(stream_key, extent, deviation, reach, cuts=(), kind=jnp.bfloat16):
    values = deviation * jax.random.normal(stream_key, extent, jnp.float32)
    if cuts:
        values = values * level_of(stream_key, extent, cuts, -0.22, 0.18)
    return jnp.clip(values, -reach, reach).astype(kind)


def setup_inputs(seed: int = 0) -> dict:
    splits = jax.random.split(jax.random.key(seed), 7)
    return {
        "history": gaussian(splits[0], (NTX, NTY, DMAX, B, P_SIZE), 1.0, 6.0, ((0, 8), (1, 4))),
        "incident": gaussian(splits[1], (NTX, NTY, STEPS, B, P_SIZE), 1.0, 6.0, ((0, 8), (1, 4)), jnp.float32),
        "blocks": gaussian(splits[2], (NTX, NTY, NBLK, B, B), (NBLK * B) ** -0.5, 0.09375, ((0, 8), (1, 4))),
        "self_inverse": draw_self_inverse(jax.random.fold_in(splits[6], 71), 0),
        "neighbour": plant(jax.random.randint(splits[4], (NTX, NTY, NBLK), 0, 9), jax.random.fold_in(splits[4], 1), 0, 8).astype(jnp.int32),
        "delay": plant(jax.random.randint(splits[5], (NTX, NTY, NBLK), 1, DMAX + 1), jax.random.fold_in(splits[5], 1), 1, DMAX).astype(jnp.int32),
    }


def reference(history, incident, blocks, self_inverse, neighbour, delay):
    past = jnp.flip(history, axis=2)
    padded = jnp.pad(past, ((1, 1), (1, 1), (0, 0), (0, 0), (0, 0)))
    frames = [padded]
    results = []
    columns = jnp.arange(NTY, dtype=jnp.int32)[:, None]
    for step in range(STEPS):
        stack = jnp.concatenate(frames, axis=2)
        slots = (step - delay + DMAX).astype(jnp.int32)

        def one_row(row):
            near = lax.dynamic_slice_in_dim(stack, row, 3, 0)
            ids = neighbour[row]
            sources = near[ids // 3, columns + ids % 3, slots[row]]
            field = jnp.einsum("yjab,yjbp->yap", blocks[row].astype(jnp.float32), sources.astype(jnp.float32))
            rhs = incident[row, :, step] - field
            solved = jnp.einsum("yab,ybp->yap", self_inverse[row], rhs, precision=lax.Precision.HIGHEST)
            return solved.astype(jnp.bfloat16)

        current = lax.map(one_row, jnp.arange(NTX, dtype=jnp.int32))
        results.append(current)
        frames.append(jnp.pad(current, ((1, 1), (1, 1), (0, 0), (0, 0)))[:, :, None])
    return jnp.stack(results, axis=2)
```

```python
import functools

import jax
import jax.numpy as jnp
from jax import lax
from jax.experimental import pallas as pl
from jax.experimental.pallas import tpu as pltpu
from jax.sharding import PartitionSpec as P

MESH = pl.DeviceIdType.MESH
LANES = 128
GROUP = 4


def kernel(
    rows,
    cols,
    near_ref,
    lag_ref,
    history,
    incident,
    blocks,
    inverse,
    out,
    hown,
    inc,
    mats,
    inv,
    hrecv,
    frecv,
    stack,
    fresh,
    load_sem,
    out_sem,
    send_sem,
    recv_sem,
):
    steps, basis, ports = incident.shape
    depth = history.shape[0]
    nblk = blocks.shape[0]
    chunks = ports // LANES
    items = chunks * steps
    slots = depth + steps - 1
    r = lax.axis_index("px")
    c = lax.axis_index("py")
    has_up, has_down = r > 0, r < rows - 1
    has_left, has_right = c > 0, c < cols - 1
    up, down, left, right = (r - 1, c), (r + 1, c), (r, c - 1), (r, c + 1)

    barrier = pltpu.get_barrier_semaphore()
    for here, peer in ((has_up, up), (has_down, down), (has_left, left), (has_right, right)):

        @pl.when(here)
        def _():
            pl.semaphore_signal(barrier, inc=1, device_id=peer, device_id_type=MESH)

    loads = []
    for k in range(chunks):
        loads.append(
            pltpu.make_async_copy(
                history.at[:, :, pl.ds(k * LANES, LANES)], hown.at[k], load_sem.at[k]
            )
        )
    loads.append(pltpu.make_async_copy(blocks, mats, load_sem.at[chunks]))
    loads.append(pltpu.make_async_copy(inverse, inv, load_sem.at[chunks + 1]))
    for k in range(chunks):
        loads.append(
            pltpu.make_async_copy(
                incident.at[:, :, pl.ds(k * LANES, LANES)], inc.at[k], load_sem.at[chunks + 2 + k]
            )
        )
    for load in loads:
        load.start()

    def copy(src, dst, item, way, slot, peer):
        return pltpu.make_async_remote_copy(
            src_ref=src,
            dst_ref=dst,
            send_sem=send_sem.at[item * 8 + way],
            recv_sem=recv_sem.at[item * 9 + slot],
            device_id=peer,
            device_id_type=MESH,
        )

    def own_ways():
        return (
            (0, has_down, down, 1),
            (1, has_up, up, 7),
            (2, has_right, right, 3),
            (3, has_left, left, 5),
        )

    def relay_ways():
        return (
            (4, has_up, 1, has_right, right, 0),
            (5, has_up, 1, has_left, left, 2),
            (6, has_down, 7, has_right, right, 6),
            (7, has_down, 7, has_left, left, 8),
        )

    def send(src, buffer, part, item):
        for way, here, peer, slot in own_ways():

            @pl.when(here)
            def _():
                copy(src, buffer.at[part, slot], item, way, slot, peer).start()

    def landed(buffer, part, item, slot):
        copy(buffer.at[part, slot], buffer.at[part, slot], item, 0, slot, up).wait_recv()

    def relay(buffer, part, item):
        for here, slot in ((has_up, 1), (has_down, 7)):

            @pl.when(here)
            def _():
                landed(buffer, part, item, slot)
                for way, _a, source, side, peer, target in relay_ways():
                    if source == slot:

                        @pl.when(side)
                        def _():
                            copy(
                                buffer.at[part, source],
                                buffer.at[part, target],
                                item,
                                way,
                                target,
                                peer,
                            ).start()

    def stencil():
        both = jnp.logical_and
        return (
            (0, both(has_up, has_left)),
            (1, has_up),
            (2, both(has_up, has_right)),
            (3, has_left),
            (5, has_right),
            (6, both(has_down, has_left)),
            (7, has_down),
            (8, both(has_down, has_right)),
        )

    for slot, here in stencil():

        @pl.when(jnp.logical_not(here))
        def _():
            def clear(i, carry):
                stack[i * 9 + slot] = jnp.zeros((basis, LANES), stack.dtype)
                return carry

            lax.fori_loop(0, chunks * slots, clear, 0)

    degree = (
        has_up.astype(jnp.int32)
        + has_down.astype(jnp.int32)
        + has_left.astype(jnp.int32)
        + has_right.astype(jnp.int32)
    )
    pl.semaphore_wait(barrier, degree)

    for k in range(chunks):
        loads[k].wait()
        send(hown.at[k], hrecv, k, k)
    for load in loads[chunks:]:
        load.wait()
    for k in range(chunks):
        for d in range(depth):
            stack[(k * slots + d) * 9 + 4] = hown[k, d]
    relay(hrecv, 0, 0)

    def body(q, carry):
        s = q // chunks
        k = q - s * chunks

        @pl.when(q + 1 < chunks)
        def _():
            relay(hrecv, q + 1, q + 1)

        @pl.when(jnp.logical_and(q + 1 >= chunks, q + 1 < items))
        def _():
            relay(frecv, q + 1 - chunks, q + 1)

        @pl.when(q < chunks)
        def _():
            for slot, here in stencil():

                @pl.when(here)
                def _():
                    if slot not in (1, 7):
                        landed(hrecv, q, q, slot)
                    for d in range(depth):
                        stack[(k * slots + d) * 9 + slot] = hrecv[q, slot, d]

        @pl.when(q >= chunks)
        def _():
            for slot, here in stencil():

                @pl.when(here)
                def _():
                    if slot not in (1, 7):
                        landed(frecv, q - chunks, q, slot)
                    stack[(k * slots + depth + s - 1) * 9 + slot] = frecv[q - chunks, slot]

        field = jnp.zeros((basis, LANES), jnp.float32)
        for j in range(0, nblk, GROUP):
            sources = []
            for i in range(j, j + GROUP):
                lag = jnp.maximum(lag_ref[i], 1)
                frame = jnp.where(s < lag, lag - s - 1, depth + s - lag)
                sources.append(stack[(k * slots + frame) * 9 + near_ref[i]])
            field = field + jnp.dot(
                jnp.concatenate([mats[i] for i in range(j, j + GROUP)], axis=1),
                jnp.concatenate(sources, axis=0),
                preferred_element_type=jnp.float32,
            )
        rhs = inc[k, s] - field
        current = jnp.dot(
            inv[...], rhs, precision=lax.Precision.HIGHEST, preferred_element_type=jnp.float32
        ).astype(jnp.bfloat16)
        fresh[q] = current

        @pl.when(s + 1 < steps)
        def _():
            stack[(k * slots + depth + s) * 9 + 4] = current
            send(fresh.at[q], frecv, q, q + chunks)

        pltpu.make_async_copy(
            fresh.at[q],
            out.at[s, :, pl.ds(pl.multiple_of(k * LANES, LANES), LANES)],
            out_sem.at[q],
        ).start()
        return carry

    lax.fori_loop(0, items, body, 0)

    def finish(q, carry):
        s = q // chunks
        k = q - s * chunks
        pltpu.make_async_copy(
            fresh.at[q],
            out.at[s, :, pl.ds(pl.multiple_of(k * LANES, LANES), LANES)],
            out_sem.at[q],
        ).wait()

        def drain(src, dst):
            for way, here, peer, slot in own_ways():

                @pl.when(here)
                def _():
                    copy(src, dst.at[slot], q, way, slot, peer).wait_send()

            for way, here, source, side, peer, target in relay_ways():

                @pl.when(jnp.logical_and(here, side))
                def _():
                    copy(dst.at[source], dst.at[target], q, way, target, peer).wait_send()

        @pl.when(q < chunks)
        def _():
            drain(hown.at[q], hrecv.at[q])

        @pl.when(q >= chunks)
        def _():
            drain(fresh.at[q - chunks], frecv.at[q - chunks])

        return carry

    lax.fori_loop(0, items, finish, 0)


def local(rows, cols, history, incident, blocks, self_inverse, neighbour, delay):
    depth, basis, ports = history.shape[2:]
    steps = incident.shape[2]
    nblk = blocks.shape[2]
    chunks = ports // LANES
    items = chunks * steps
    slots = depth + steps - 1
    later = items - chunks
    smem = pl.BlockSpec(memory_space=pltpu.SMEM)
    hbm = pl.BlockSpec(memory_space=pl.ANY)
    half = jnp.bfloat16
    currents = pl.pallas_call(
        functools.partial(kernel, rows, cols),
        out_shape=jax.ShapeDtypeStruct((steps, basis, ports), half),
        in_specs=[smem, smem, hbm, hbm, hbm, hbm],
        out_specs=hbm,
        scratch_shapes=[
            pltpu.VMEM((chunks, depth, basis, LANES), half),
            pltpu.VMEM((chunks, steps, basis, LANES), jnp.float32),
            pltpu.VMEM((nblk, basis, basis), half),
            pltpu.VMEM((basis, basis), jnp.float32),
            pltpu.VMEM((chunks, 9, depth, basis, LANES), half),
            pltpu.VMEM((later, 9, basis, LANES), half),
            pltpu.VMEM((chunks * slots * 9, basis, LANES), half),
            pltpu.VMEM((items, basis, LANES), half),
            pltpu.SemaphoreType.DMA((2 * chunks + 2,)),
            pltpu.SemaphoreType.DMA((items,)),
            pltpu.SemaphoreType.DMA((items * 8,)),
            pltpu.SemaphoreType.DMA((items * 9,)),
        ],
        compiler_params=pltpu.CompilerParams(
            collective_id=0, has_side_effects=True, vmem_limit_bytes=48 * 1024 * 1024
        ),
    )(
        neighbour[0, 0],
        delay[0, 0],
        history[0, 0],
        incident[0, 0],
        blocks[0, 0],
        self_inverse[0, 0],
    )
    return currents[None, None]


def solution(mesh):
    in_specs = (
        P("px", "py", None, None, None),
        P("px", "py", None, None, None),
        P("px", "py", None, None, None),
        P("px", "py", None, None),
        P("px", "py", None),
        P("px", "py", None),
    )
    out_specs = P("px", "py", None, None, None)
    body = functools.partial(local, mesh.shape["px"], mesh.shape["py"])
    return jax.shard_map(body, mesh=mesh, in_specs=in_specs, out_specs=out_specs, check_vma=False)
```

```python
import functools

import jax
import jax.numpy as jnp
from jax import lax
from jax.experimental import pallas as pl
from jax.experimental.pallas import tpu as pltpu
from jax.sharding import PartitionSpec as P

MESH = pl.DeviceIdType.MESH
LANES = 128
GROUP = 4


ROW, ROW_LAG, COLUMN_LAG, WORK = 1.5, 2.5, 3.0, 1.0


def order(chunks, depth, steps):
    now, row_free = 0.0, 0.0
    ready, done, result = [], {}, []

    def launch(k, t):
        nonlocal row_free
        row_free = max(row_free, now) + ROW
        ready.append((row_free + ROW_LAG, "relay", k, t))

    def start(k):
        for t in range(depth):
            result.append(("send", k, t))
            launch(k, t)

    start(0)
    if chunks > 1:
        start(1)
    pending = list(range(2, chunks))
    while ready:
        ready.sort()
        at, kind, k, t = ready.pop(0)
        now = max(now, at)
        result.append((kind, k, t))
        if kind == "relay":
            if t >= depth - 1:
                ready.append((now + COLUMN_LAG, "compute", k, t - depth + 1))
        else:
            now += WORK
            if t + 1 < steps:
                launch(k, depth + t)
            if pending:
                start(pending.pop(0))
    return result


def kernel(
    rows,
    cols,
    near_ref,
    lag_ref,
    history,
    incident,
    blocks,
    inverse,
    out,
    hown,
    inc,
    mats,
    inv,
    split,
    recv,
    stack,
    fresh,
    load_sem,
    out_sem,
    send_sem,
    recv_sem,
):
    steps, basis, ports = incident.shape
    depth = history.shape[0]
    nblk = blocks.shape[0]
    chunks = ports // LANES
    slots = depth + steps - 1
    r = lax.axis_index("px")
    c = lax.axis_index("py")
    has_up, has_down = r > 0, r < rows - 1
    has_left, has_right = c > 0, c < cols - 1
    up, down, left, right = (r - 1, c), (r + 1, c), (r, c - 1), (r, c + 1)

    barrier = pltpu.get_barrier_semaphore()
    for here, peer in ((has_up, up), (has_down, down), (has_left, left), (has_right, right)):

        @pl.when(here)
        def _():
            pl.semaphore_signal(barrier, inc=1, device_id=peer, device_id_type=MESH)

    loads = []
    for k in range(chunks):
        loads.append(
            pltpu.make_async_copy(
                history.at[:, :, pl.ds(k * LANES, LANES)], hown.at[k], load_sem.at[k]
            )
        )
    loads.append(pltpu.make_async_copy(blocks, mats, load_sem.at[chunks]))
    loads.append(pltpu.make_async_copy(inverse, inv, load_sem.at[chunks + 1]))
    for k in range(chunks):
        loads.append(
            pltpu.make_async_copy(
                incident.at[:, :, pl.ds(k * LANES, LANES)], inc.at[k], load_sem.at[chunks + 2 + k]
            )
        )
    for load in loads:
        load.start()

    def copy(src, dst, item, way, slot, peer):
        return pltpu.make_async_remote_copy(
            src_ref=src,
            dst_ref=dst,
            send_sem=send_sem.at[item * 8 + way],
            recv_sem=recv_sem.at[item * 9 + slot],
            device_id=peer,
            device_id_type=MESH,
        )

    own_ways = (
        (0, has_down, down, 1),
        (1, has_up, up, 7),
        (2, has_right, right, 3),
        (3, has_left, left, 5),
    )
    relay_ways = (
        (4, has_up, 1, has_right, right, 0),
        (5, has_up, 1, has_left, left, 2),
        (6, has_down, 7, has_right, right, 6),
        (7, has_down, 7, has_left, left, 8),
    )
    both = jnp.logical_and
    stencil = (
        (0, both(has_up, has_left)),
        (1, has_up),
        (2, both(has_up, has_right)),
        (3, has_left),
        (5, has_right),
        (6, both(has_down, has_left)),
        (7, has_down),
        (8, both(has_down, has_right)),
    )

    def send(src, item):
        for way, here, peer, slot in own_ways:

            @pl.when(here)
            def _():
                copy(src, recv.at[item, slot], item, way, slot, peer).start()

    def landed(item, slot):
        copy(recv.at[item, slot], recv.at[item, slot], item, 0, slot, up).wait_recv()

    def relay(item):
        for here, slot in ((has_up, 1), (has_down, 7)):

            @pl.when(here)
            def _():
                landed(item, slot)
                for way, _a, source, side, peer, target in relay_ways:
                    if source == slot:

                        @pl.when(side)
                        def _():
                            copy(
                                recv.at[item, source],
                                recv.at[item, target],
                                item,
                                way,
                                target,
                                peer,
                            ).start()

    def gather(item):
        for slot, here in stencil:

            @pl.when(here)
            def _():
                if slot not in (1, 7):
                    landed(item, slot)
                stack[item * 9 + slot] = recv[item, slot]

    def output(k, s):
        return pltpu.make_async_copy(
            fresh.at[k, s], out.at[s, :, pl.ds(k * LANES, LANES)], out_sem.at[k * steps + s]
        )

    def compute(k, s):
        if s == 0:
            for t in range(depth):
                gather(k * slots + t)
        else:
            gather(k * slots + depth + s - 1)
        field = jnp.zeros((basis, LANES), jnp.float32)
        for j in range(0, nblk, GROUP):
            sources = []
            for i in range(j, j + GROUP):
                lag = jnp.maximum(lag_ref[i], 1)
                frame = jnp.where(s < lag, lag - s - 1, depth + s - lag)
                sources.append(stack[(k * slots + frame) * 9 + near_ref[i]])
            field = field + jnp.dot(
                jnp.concatenate([mats[i] for i in range(j, j + GROUP)], axis=1),
                jnp.concatenate(sources, axis=0),
                preferred_element_type=jnp.float32,
            )
        rhs = inc[k, s] - field
        high = rhs.astype(jnp.bfloat16)
        low = (rhs - high.astype(jnp.float32)).astype(jnp.bfloat16)
        current = jnp.dot(
            split[...],
            jnp.concatenate([high, low, high], axis=0),
            preferred_element_type=jnp.float32,
        ).astype(jnp.bfloat16)
        fresh[k, s] = current
        if s + 1 < steps:
            item = k * slots + depth + s
            send(fresh.at[k, s], item)
            stack[item * 9 + 4] = current
        output(k, s).start()

    degree = (
        has_up.astype(jnp.int32)
        + has_down.astype(jnp.int32)
        + has_left.astype(jnp.int32)
        + has_right.astype(jnp.int32)
    )
    pl.semaphore_wait(barrier, degree)

    first = True
    for kind, k, t in order(chunks, depth, steps):
        item = k * slots + t
        if kind == "send":
            if t == 0:
                loads[k].wait()
            send(hown.at[k, t], item)
        if kind == "relay":
            if first:
                first = False
                for slot, here in stencil:

                    @pl.when(jnp.logical_not(here))
                    def _():
                        def clear(i, carry):
                            stack[i * 9 + slot] = jnp.zeros((basis, LANES), stack.dtype)
                            return carry

                        lax.fori_loop(0, chunks * slots, clear, 0)

                for load in loads[chunks:]:
                    load.wait()
                whole = inv[...]
                high = whole.astype(jnp.bfloat16)
                low = (whole - high.astype(jnp.float32)).astype(jnp.bfloat16)
                split[...] = jnp.concatenate([high, high, low], axis=1)
            relay(item)
        if kind == "compute":
            if t == 0:
                for d in range(depth):
                    stack[(k * slots + d) * 9 + 4] = hown[k, d]
            compute(k, t)

    for k in range(chunks):
        for s in range(steps):
            output(k, s).wait()

    def finish(item, carry):
        for way, here, peer, slot in own_ways:

            @pl.when(here)
            def _():
                copy(fresh.at[0, 0], recv.at[item, slot], item, way, slot, peer).wait_send()

        for way, here, source, side, peer, target in relay_ways:

            @pl.when(both(here, side))
            def _():
                copy(
                    recv.at[item, source], recv.at[item, target], item, way, target, peer
                ).wait_send()

        return carry

    lax.fori_loop(0, chunks * slots, finish, 0)


def local(rows, cols, history, incident, blocks, self_inverse, neighbour, delay):
    depth, basis, ports = history.shape[2:]
    steps = incident.shape[2]
    nblk = blocks.shape[2]
    chunks = ports // LANES
    items = chunks * steps
    slots = depth + steps - 1
    smem = pl.BlockSpec(memory_space=pltpu.SMEM)
    hbm = pl.BlockSpec(memory_space=pltpu.HBM)
    half = jnp.bfloat16
    currents = pl.pallas_call(
        functools.partial(kernel, rows, cols),
        out_shape=jax.ShapeDtypeStruct((steps, basis, ports), half),
        in_specs=[smem, smem, hbm, hbm, hbm, hbm],
        out_specs=pl.BlockSpec(memory_space=pl.ANY),
        scratch_shapes=[
            pltpu.VMEM((chunks, depth, basis, LANES), half),
            pltpu.VMEM((chunks, steps, basis, LANES), jnp.float32),
            pltpu.VMEM((nblk, basis, basis), half),
            pltpu.VMEM((basis, basis), jnp.float32),
            pltpu.VMEM((basis, 3 * basis), half),
            pltpu.VMEM((chunks * slots, 9, basis, LANES), half),
            pltpu.VMEM((chunks * slots * 9, basis, LANES), half),
            pltpu.VMEM((chunks, steps, basis, LANES), half),
            pltpu.SemaphoreType.DMA((2 * chunks + 2,)),
            pltpu.SemaphoreType.DMA((items,)),
            pltpu.SemaphoreType.DMA((chunks * slots * 8,)),
            pltpu.SemaphoreType.DMA((chunks * slots * 9,)),
        ],
        compiler_params=pltpu.CompilerParams(
            collective_id=0, has_side_effects=True, vmem_limit_bytes=48 * 1024 * 1024
        ),
    )(
        neighbour[0, 0],
        delay[0, 0],
        history[0, 0],
        incident[0, 0],
        blocks[0, 0],
        self_inverse[0, 0],
    )
    return currents[None, None]


def solution(mesh):
    in_specs = (
        P("px", "py", None, None, None),
        P("px", "py", None, None, None),
        P("px", "py", None, None, None),
        P("px", "py", None, None),
        P("px", "py", None),
        P("px", "py", None),
    )
    out_specs = P("px", "py", None, None, None)
    body = functools.partial(local, mesh.shape["px"], mesh.shape["py"])
    return jax.shard_map(body, mesh=mesh, in_specs=in_specs, out_specs=out_specs, check_vma=False)
```

```python
import functools

import jax
import jax.numpy as jnp
from jax import lax
from jax.experimental import pallas as pl
from jax.experimental.pallas import tpu as pltpu
from jax.sharding import PartitionSpec as P

MESH = pl.DeviceIdType.MESH
LANES = 128
GROUP = 4


def kernel(
    rows,
    cols,
    near_ref,
    lag_ref,
    history,
    incident,
    blocks,
    inverse,
    out,
    hown,
    inc,
    mats,
    inv,
    split,
    hrecv,
    frecv,
    stack,
    fresh,
    load_sem,
    out_sem,
    send_sem,
    recv_sem,
):
    steps, basis, ports = incident.shape
    depth = history.shape[0]
    nblk = blocks.shape[0]
    chunks = ports // LANES
    items = chunks * steps
    slots = depth + steps - 1
    r = lax.axis_index("px")
    c = lax.axis_index("py")
    has_up, has_down = r > 0, r < rows - 1
    has_left, has_right = c > 0, c < cols - 1
    up, down, left, right = (r - 1, c), (r + 1, c), (r, c - 1), (r, c + 1)

    barrier = pltpu.get_barrier_semaphore()
    for here, peer in ((has_up, up), (has_down, down), (has_left, left), (has_right, right)):

        @pl.when(here)
        def _():
            pl.semaphore_signal(barrier, inc=1, device_id=peer, device_id_type=MESH)

    loads = []
    for k in range(chunks):
        loads.append(
            pltpu.make_async_copy(
                history.at[:, :, pl.ds(k * LANES, LANES)], hown.at[k], load_sem.at[k]
            )
        )
    loads.append(pltpu.make_async_copy(blocks, mats, load_sem.at[chunks]))
    loads.append(pltpu.make_async_copy(inverse, inv, load_sem.at[chunks + 1]))
    for k in range(chunks):
        loads.append(
            pltpu.make_async_copy(
                incident.at[:, :, pl.ds(k * LANES, LANES)], inc.at[k], load_sem.at[chunks + 2 + k]
            )
        )
    for load in loads:
        load.start()

    def copy(src, dst, item, way, slot, peer):
        return pltpu.make_async_remote_copy(
            src_ref=src,
            dst_ref=dst,
            send_sem=send_sem.at[item * 8 + way],
            recv_sem=recv_sem.at[item * 9 + slot],
            device_id=peer,
            device_id_type=MESH,
        )

    def own_ways():
        return (
            (2, has_right, right, 3),
            (3, has_left, left, 5),
            (0, has_down, down, 1),
            (1, has_up, up, 7),
        )

    def relay_ways():
        return (
            (4, has_up, 1, has_right, right, 0),
            (5, has_up, 1, has_left, left, 2),
            (6, has_down, 7, has_right, right, 6),
            (7, has_down, 7, has_left, left, 8),
        )

    def send(src, buffer, part, item):
        for way, here, peer, slot in own_ways():

            @pl.when(here)
            def _():
                copy(src, buffer.at[part, slot], item, way, slot, peer).start()

    def landed(buffer, part, item, slot):
        copy(buffer.at[part, slot], buffer.at[part, slot], item, 0, slot, up).wait_recv()

    def relay(buffer, part, item):
        for here, slot in ((has_up, 1), (has_down, 7)):

            @pl.when(here)
            def _():
                landed(buffer, part, item, slot)
                for way, _a, source, side, peer, target in relay_ways():
                    if source == slot:

                        @pl.when(side)
                        def _():
                            copy(
                                buffer.at[part, source],
                                buffer.at[part, target],
                                item,
                                way,
                                target,
                                peer,
                            ).start()

    def stencil():
        both = jnp.logical_and
        return (
            (0, both(has_up, has_left)),
            (1, has_up),
            (2, both(has_up, has_right)),
            (3, has_left),
            (5, has_right),
            (6, both(has_down, has_left)),
            (7, has_down),
            (8, both(has_down, has_right)),
        )

    for slot, here in stencil():

        @pl.when(jnp.logical_not(here))
        def _():
            def clear(i, carry):
                stack[i * 9 + slot] = jnp.zeros((basis, LANES), stack.dtype)
                return carry

            lax.fori_loop(0, chunks * slots, clear, 0)

    degree = (
        has_up.astype(jnp.int32)
        + has_down.astype(jnp.int32)
        + has_left.astype(jnp.int32)
        + has_right.astype(jnp.int32)
    )
    pl.semaphore_wait(barrier, degree)

    for k in range(chunks):
        loads[k].wait()
        send(hown.at[k], hrecv, k, k)
    for load in loads[chunks:]:
        load.wait()
    whole = inv[...]
    high = whole.astype(jnp.bfloat16)
    low = (whole - high.astype(jnp.float32)).astype(jnp.bfloat16)
    split[...] = jnp.concatenate([high, high, low], axis=1)
    for k in range(chunks):
        for d in range(depth):
            stack[(k * slots + d) * 9 + 4] = hown[k, d]
    for k in range(chunks):
        relay(hrecv, k, k)

    def body(q, carry):
        s = q // chunks
        k = q - s * chunks

        @pl.when(jnp.logical_and(q >= chunks, k == 0))
        def _():
            for later in range(chunks):
                relay(frecv, q - chunks + later, q + later)

        @pl.when(q < chunks)
        def _():
            for slot, here in stencil():

                @pl.when(here)
                def _():
                    if slot not in (1, 7):
                        landed(hrecv, q, q, slot)
                    for d in range(depth):
                        stack[(k * slots + d) * 9 + slot] = hrecv[q, slot, d]

        @pl.when(q >= chunks)
        def _():
            for slot, here in stencil():

                @pl.when(here)
                def _():
                    if slot not in (1, 7):
                        landed(frecv, q - chunks, q, slot)
                    stack[(k * slots + depth + s - 1) * 9 + slot] = frecv[q - chunks, slot]

        field = jnp.zeros((basis, LANES), jnp.float32)
        for j in range(0, nblk, GROUP):
            sources = []
            for i in range(j, j + GROUP):
                lag = jnp.maximum(lag_ref[i], 1)
                frame = jnp.where(s < lag, lag - s - 1, depth + s - lag)
                sources.append(stack[(k * slots + frame) * 9 + near_ref[i]])
            field = field + jnp.dot(
                jnp.concatenate([mats[i] for i in range(j, j + GROUP)], axis=1),
                jnp.concatenate(sources, axis=0),
                preferred_element_type=jnp.float32,
            )
        rhs = inc[k, s] - field
        high = rhs.astype(jnp.bfloat16)
        low = (rhs - high.astype(jnp.float32)).astype(jnp.bfloat16)
        current = jnp.dot(
            split[...],
            jnp.concatenate([high, low, high], axis=0),
            preferred_element_type=jnp.float32,
        ).astype(jnp.bfloat16)
        fresh[q] = current

        @pl.when(s + 1 < steps)
        def _():
            stack[(k * slots + depth + s) * 9 + 4] = current
            send(fresh.at[q], frecv, q, q + chunks)

        pltpu.make_async_copy(
            fresh.at[q],
            out.at[s, :, pl.ds(pl.multiple_of(k * LANES, LANES), LANES)],
            out_sem.at[q],
        ).start()
        return carry

    lax.fori_loop(0, items, body, 0)

    def finish(q, carry):
        s = q // chunks
        k = q - s * chunks
        pltpu.make_async_copy(
            fresh.at[q],
            out.at[s, :, pl.ds(pl.multiple_of(k * LANES, LANES), LANES)],
            out_sem.at[q],
        ).wait()

        def drain(src, dst):
            for way, here, peer, slot in own_ways():

                @pl.when(here)
                def _():
                    copy(src, dst.at[slot], q, way, slot, peer).wait_send()

            for way, here, source, side, peer, target in relay_ways():

                @pl.when(jnp.logical_and(here, side))
                def _():
                    copy(dst.at[source], dst.at[target], q, way, target, peer).wait_send()

        @pl.when(q < chunks)
        def _():
            drain(hown.at[q], hrecv.at[q])

        @pl.when(q >= chunks)
        def _():
            drain(fresh.at[q - chunks], frecv.at[q - chunks])

        return carry

    lax.fori_loop(0, items, finish, 0)


def local(rows, cols, history, incident, blocks, self_inverse, neighbour, delay):
    depth, basis, ports = history.shape[2:]
    steps = incident.shape[2]
    nblk = blocks.shape[2]
    chunks = ports // LANES
    items = chunks * steps
    slots = depth + steps - 1
    later = items - chunks
    smem = pl.BlockSpec(memory_space=pltpu.SMEM)
    hbm = pl.BlockSpec(memory_space=pltpu.HBM)
    half = jnp.bfloat16
    currents = pl.pallas_call(
        functools.partial(kernel, rows, cols),
        out_shape=jax.ShapeDtypeStruct((steps, basis, ports), half),
        in_specs=[smem, smem, hbm, hbm, hbm, hbm],
        out_specs=pl.BlockSpec(memory_space=pl.ANY),
        scratch_shapes=[
            pltpu.VMEM((chunks, depth, basis, LANES), half),
            pltpu.VMEM((chunks, steps, basis, LANES), jnp.float32),
            pltpu.VMEM((nblk, basis, basis), half),
            pltpu.VMEM((basis, basis), jnp.float32),
            pltpu.VMEM((basis, 3 * basis), half),
            pltpu.VMEM((chunks, 9, depth, basis, LANES), half),
            pltpu.VMEM((later, 9, basis, LANES), half),
            pltpu.VMEM((chunks * slots * 9, basis, LANES), half),
            pltpu.VMEM((items, basis, LANES), half),
            pltpu.SemaphoreType.DMA((2 * chunks + 2,)),
            pltpu.SemaphoreType.DMA((items,)),
            pltpu.SemaphoreType.DMA((items * 8,)),
            pltpu.SemaphoreType.DMA((items * 9,)),
        ],
        compiler_params=pltpu.CompilerParams(
            collective_id=0, has_side_effects=True, vmem_limit_bytes=48 * 1024 * 1024
        ),
    )(
        neighbour[0, 0],
        delay[0, 0],
        history[0, 0],
        incident[0, 0],
        blocks[0, 0],
        self_inverse[0, 0],
    )
    return currents[None, None]


def solution(mesh):
    in_specs = (
        P("px", "py", None, None, None),
        P("px", "py", None, None, None),
        P("px", "py", None, None, None),
        P("px", "py", None, None),
        P("px", "py", None),
        P("px", "py", None),
    )
    out_specs = P("px", "py", None, None, None)
    body = functools.partial(local, mesh.shape["px"], mesh.shape["py"])
    return jax.shard_map(body, mesh=mesh, in_specs=in_specs, out_specs=out_specs, check_vma=False)
```
